32 devices in a mesh: section: 4 (over y, x), space: 8 (over z, core).
Axes of the slice: x: 2, y: 2, z: 4, core: 2. Of those that a mesh axis runs over, the one named last changes fastest.
Arguments:
- start_state: float32 [8, 6, 64, 512], P(None, None, 'space'), may hold values from -6 to 6
- stiffness: float32 [2, 64, 512], P(None, 'space'), may hold values from 0.5 to 4
- contact_a: int32 [8, 8, 8], P('section', 'space'), may hold values from 0 to 31
- contact_b: int32 [8, 8, 8], P('section', 'space'), may hold values from 0 to 39
- pair_count: int32 [8, 8], P('section', 'space'), may hold values from 1 to 8, 36 in all within a row
- cotangent: float32 [8, 6, 64, 512], P(None, None, 'space'), may hold values from -6 to 6
Outputs:
- exit_state: float32 [4, 8, 6, 64, 512], P('section', None, None, 'space')
- incoming_state_gradient: float32 [4, 8, 6, 64, 512], P('section', None, None, 'space')
- stiffness_grad: float32 [2, 64, 512], P(None, 'space')
The draws below stay inside these ranges and needn't reach their ends.
Inputs may be any that keep to these rules, and one draw needn't show every extreme that they name: Tiles are numbered within one device's band: contact_a over its own 8 rows, contact_b over those rows with one row added above and below, the upper added row first. Slots at or beyond pair_count are ignored; at every step some device has all 8 slots live.
All inputs are finite; a program needn't handle non-finite values.
Results may differ from the reference program's by a relative error of at most 0.0003.
Values sent between devices are 32-bit elements; how exact they have to be, the bound alone decides.
A program may use at most 64 MiB of HBM per device.

```python
import math
import jax
import jax.numpy as jnp
import numpy as np
from jax import lax

COLS = 512
MICRO = 8
SECTION_STEPS = 2
PAIRS = 8
ROWS = 64
STEPS = 8
TILES_DEV = 32
N_SECTION = 4
N_SPACE = 8


def set_ends(result, key, low, largest):
    longest = result.shape.index(max(result.shape))
    spots = []
    for shift in (0, 1):
        where = [jax.random.randint(jax.random.fold_in(key, axis), (), 0, length) for axis, length in enumerate(result.shape)]
        where[longest] = (where[longest] + shift) % result.shape[longest]
        spots.append(tuple(where))
    return result.at[spots[0]].set(low).at[spots[1]].set(largest)


def level_of(rng, extent, cuts, smallest, largest):
    loudness, own = 1.0, jax.random.fold_in(rng, 6)
    for dim, parts in cuts:
        steps = jnp.exp(jax.random.uniform(jax.random.fold_in(own, dim), (parts,), jnp.float32, smallest / len(cuts), largest / len(cuts)))
        loudness = loudness * jnp.repeat(steps, extent[dim] // parts).reshape([-1 if axis == dim else 1 for axis in range(len(extent))])
    return loudness


def profile(number_of, total, limit, lean):
    portions = [(1 << 20) // math.isqrt(standing ** lean) + 1 for standing in range(2, number_of + 1)]
    spare, holding = total - limit - (number_of - 1), [1] * (number_of - 1)
    while spare > 0:
        movable = [i for i in range(number_of - 1) if holding[i] < limit]
        mass, budget = sum([portions[i] for i in movable]), spare
        for i in movable:
            extra = min(limit - holding[i], max(1, budget * portions[i] // mass), spare)
            holding[i] = holding[i] + extra
            spare = spare - extra
    return np.array([limit] + holding)


def ragged(rng, amount, total, most, skew):
    if amount == 2:
        one = jax.random.randint(rng, (), max(1, total - most), min(most, total - 1) + 1)
        return jnp.stack([one, total - one])
    sizes = jnp.asarray(profile(amount, total, most, skew), jnp.int32)
    pairs = (amount - 1) // 2
    giver, sink = sizes[1:1 + 2 * pairs:2], sizes[2:2 + 2 * pairs:2]
    room = jnp.minimum(giver - 1, most - sink)
    shifted = jax.random.randint(jax.random.fold_in(rng, 1), (pairs,), 0, 1 << 20) % (room + 1)
    sizes = sizes.at[1:1 + 2 * pairs:2].set(giver - shifted).at[2:2 + 2 * pairs:2].set(sink + shifted)
    return sizes[jax.random.permutation(jax.random.fold_in(rng, 2), amount)]


def scatter_about(stream_key, dims, width, reach, shards=(), held_as=jnp.bfloat16):
    array = width * jax.random.normal(stream_key, dims, jnp.float32)
    if shards:
        array = array * level_of(stream_key, dims, shards, -0.22, 0.18)
    return jnp.clip(array, -reach, reach).astype(held_as)


def setup_inputs(seed: int = 0) -> dict:
    key_of = jax.random.split(jax.random.key(seed), 7)
    return {
        "start_state": scatter_about(key_of[0], (MICRO, 6, ROWS, COLS), 1.0, 6.0, ((2, 8),), jnp.float32),
        "stiffness": jnp.clip(jnp.exp(math.log(4.0) - 2.0794415 * jax.random.uniform(key_of[1], (2, ROWS, COLS), jnp.float32) ** level_of(key_of[1], (2, ROWS, COLS), ((1, 8),), -0.2, 0.2)), 0.5, 4.0),
        "contact_a": set_ends(jax.random.randint(key_of[2], (STEPS, N_SPACE, PAIRS), 0, TILES_DEV), jax.random.fold_in(key_of[2], 1), 0, TILES_DEV - 1).astype(jnp.int32),
        "contact_b": set_ends(jax.random.randint(key_of[3], (STEPS, N_SPACE, PAIRS), 0, TILES_DEV + 2 * COLS // 128), jax.random.fold_in(key_of[3], 1), 0, (TILES_DEV + 2 * COLS // 128) - 1).astype(jnp.int32),
        "pair_count": jax.vmap(lambda own: ragged(own, N_SPACE, (N_SPACE + 1) * PAIRS // 2, PAIRS, 2))(jax.random.split(key_of[4], STEPS)).reshape((STEPS, N_SPACE)).astype(jnp.int32),
        "cotangent": scatter_about(key_of[5], (MICRO, 6, ROWS, COLS), 1.0, 6.0, ((2, 8),), jnp.float32),
    }


time_step = 0.1
damping = 0.98
rest_length = 1.0
contact_scale = 0.3
kernel_spread = 2.0
gravity = 0.5
tiny_length = 1e-06

def spring(offset, edge_constant):
    length = jnp.sqrt(lax.optimization_barrier(jnp.sum(offset * offset, axis=0)) + tiny_length)
    return (edge_constant * (length - rest_length) / length)[None] * offset

def contact(points, extended, hits_a, hits_b, active):
    tiles_own = points.reshape(3, -1, 128)
    tiles_all = extended.reshape(3, -1, 128)
    own_points = jnp.einsum('pt,ctk->cpk', hits_a, tiles_own, precision=lax.Precision.HIGHEST)
    other_points = jnp.einsum('pt,ctk->cpk', hits_b, tiles_all, precision=lax.Precision.HIGHEST)
    separation = own_points[:, :, :, None] - other_points[:, :, None, :]
    spring_weights = jnp.exp(-lax.optimization_barrier(jnp.sum(separation * separation, axis=0)) / kernel_spread) * active[:, None, None]
    repulsion = 2.0 * contact_scale / kernel_spread * lax.optimization_barrier(jnp.sum(spring_weights[None] * separation, axis=3))
    placed = jnp.einsum('pt,cpk->ctk', hits_a, repulsion, precision=lax.Precision.HIGHEST)
    return placed.reshape(points.shape)

def local_step(extended, velocity, stiff_row, stiff_column, hits_a, hits_b, active):
    points = extended[:, 1:-1]
    row_width = points.shape[2]
    column_mask = (lax.broadcasted_iota(jnp.int32, (1, row_width), 1) < row_width - 1).astype(stiff_row.dtype)
    right_edge = stiff_row * column_mask
    left_edge = jnp.pad(right_edge[:, :-1], ((0, 0), (1, 0)))
    right_points = jnp.pad(points[:, :, 1:], ((0, 0), (0, 0), (0, 1)))
    left_points = jnp.pad(points[:, :, :-1], ((0, 0), (0, 0), (1, 0)))
    total_force = spring(right_points - points, right_edge) + spring(left_points - points, left_edge)
    total_force = total_force + spring(extended[:, :-2] - points, stiff_column[:-1])
    total_force = total_force + spring(extended[:, 2:] - points, stiff_column[1:])
    total_force = total_force + contact(points, extended, hits_a, hits_b, active)
    gravity_pull = jnp.zeros((3, 1, 1), total_force.dtype).at[2].set(-gravity)
    velocity_new = damping * (velocity + time_step * (total_force + gravity_pull))
    points_new = points + time_step * velocity_new
    return jnp.concatenate([points_new, velocity_new], axis=0)

def tables(first_tiles, second_tiles, live_count, tiles_own, tiles_all, float_type):
    slot_count = first_tiles.shape[0]
    hits_a = (first_tiles[:, None] == lax.broadcasted_iota(jnp.int32, (slot_count, tiles_own), 1)).astype(float_type)
    hits_b = (second_tiles[:, None] == lax.broadcasted_iota(jnp.int32, (slot_count, tiles_all), 1)).astype(float_type)
    active = (lax.iota(jnp.int32, slot_count) < live_count).astype(float_type)
    return (hits_a, hits_b, active)

def region_step(state_now, stiff_row, stiff_masked, first_tiles, second_tiles, live_count):
    spaces = first_tiles.shape[0]
    total_rows = state_now.shape[1]
    row_width = state_now.shape[2]
    own_rows = total_rows // spaces
    padded = jnp.pad(state_now[:3], ((0, 0), (1, 1), (0, 0)))
    column_all = jnp.concatenate([jnp.zeros((1, row_width), stiff_masked.dtype), stiff_masked], axis=0)
    checked_step = jax.checkpoint(local_step)

    def region_one(space_index):
        start_row = space_index * own_rows
        extended = lax.dynamic_slice_in_dim(padded, start_row, own_rows + 2, 1)
        velocity = lax.dynamic_slice_in_dim(state_now[3:], start_row, own_rows, 1)
        own_row = lax.dynamic_slice_in_dim(stiff_row, start_row, own_rows, 0)
        own_column = lax.dynamic_slice_in_dim(column_all, start_row, own_rows + 1, 0)
        hits_a, hits_b, active = tables(first_tiles[space_index], second_tiles[space_index], live_count[space_index], own_rows * row_width // 128, (own_rows + 2) * row_width // 128, state_now.dtype)
        return checked_step(extended, velocity, own_row, own_column, hits_a, hits_b, active)
    blocks = lax.map(region_one, jnp.arange(spaces, dtype=jnp.int32))
    return blocks.transpose(1, 0, 2, 3).reshape(6, total_rows, row_width)

def reference(start_state, stiffness, contact_a, contact_b, pair_count, cotangent):
    total_rows = stiffness.shape[1]
    row_mask = (jnp.arange(total_rows, dtype=jnp.int32) < total_rows - 1).astype(stiffness.dtype)[:, None]

    def advance(state_now, stiff_row, stiff_column, section_total):
        masked = stiff_column * row_mask
        return jax.vmap(region_step, in_axes=(0, None, None, None, None, None))(state_now, stiff_row, masked, contact_a[section_total], contact_b[section_total], pair_count[section_total])
    visited = []
    leaving_state_list = []
    state_now = start_state
    for section_ordinal in range(N_SECTION):
        for section_inner_step in range(SECTION_STEPS):
            section_total = section_ordinal * SECTION_STEPS + section_inner_step
            visited.append(state_now)
            state_now = advance(state_now, stiffness[0], stiffness[1], section_total)
        leaving_state_list.append(state_now)
    adjoint = cotangent
    grad_row = jnp.zeros_like(stiffness[0])
    grad_column = jnp.zeros_like(stiffness[1])
    adjoint_list = [None] * N_SECTION
    for section_ordinal in reversed(range(N_SECTION)):
        for section_inner_step in reversed(range(SECTION_STEPS)):
            section_total = section_ordinal * SECTION_STEPS + section_inner_step

            def forward_one(state_in, row_in, column_in, section_total=section_total):
                return advance(state_in, row_in, column_in, section_total)
            _, pullback = jax.vjp(forward_one, visited[section_total], stiffness[0], stiffness[1])
            adjoint, part_row, part_column = pullback(adjoint)
            grad_row = grad_row + part_row
            grad_column = grad_column + part_column
        adjoint_list[section_ordinal] = adjoint
    return (jnp.stack(leaving_state_list), jnp.stack(adjoint_list), jnp.stack([grad_row, grad_column]))
```

```python
import functools

import jax
import jax.numpy as jnp
from jax import lax
from jax.experimental import pallas as pl
from jax.experimental.pallas import tpu as pltpu
from jax.sharding import PartitionSpec as P

time_step = 0.1
damping = 0.98
contact_scale = 0.3
kernel_spread = 2.0
gravity = 0.5
tiny_length = 1e-06
LANES = 128
CHUNK = 32
MESH = pl.DeviceIdType.MESH


def total(parts):
    result = parts[0]
    for part in parts[1:]:
        result = result + part
    return result


def kernel(
    dims,
    start_hbm,
    stiff_ref,
    lists_ref,
    cot_hbm,
    exit_hbm,
    adj_hbm,
    grad_ref,
    lists_all,
    lists_s,
    ext,
    vel,
    adj,
    exit_buf,
    adj_buf,
    halo_out,
    halo_in,
    back_out,
    back_in,
    above_out,
    above_in,
    upper_out,
    upper_in,
    grad_parts,
    gath,
    force_adj,
    load_sem,
    smem_sem,
    list_send,
    list_recv,
    halo_send,
    halo_recv,
    back_send,
    back_recv,
    above_send,
    above_recv,
    upper_send,
    upper_recv,
    exit_send,
    exit_recv,
    adj_send,
    adj_recv,
    grad_send,
    grad_recv,
):
    sections, spaces, share, steps_section, pairs, rows, width = dims
    steps = sections * steps_section
    quarter = width // LANES
    sec = lax.axis_index("section")
    spc = lax.axis_index("space")
    has_up = spc > 0
    has_down = spc < spaces - 1

    row_id = lax.broadcasted_iota(jnp.int32, (rows, width), 0)
    lane_id = lax.broadcasted_iota(jnp.int32, (rows, width), 1)
    tile_in_row = lax.shift_right_logical(lane_id, LANES.bit_length() - 1)
    tile_id = row_id * quarter + tile_in_row
    first_row = row_id == 0
    last_row = row_id == rows - 1
    halo_tile = jnp.where(
        first_row,
        tile_in_row,
        jnp.where(row_id == 1, tile_in_row + (rows + 1) * quarter, -1),
    )

    def remote(src, dst, send, recv, device):
        return pltpu.make_async_remote_copy(
            src_ref=src,
            dst_ref=dst,
            send_sem=send,
            recv_sem=recv,
            device_id=device,
            device_id_type=MESH,
        )

    def peer(k):
        return lax.rem(sec + k, sections)

    def store_rows(ref, index, row, value):
        for q in range(quarter):
            part = value[:, q * LANES : (q + 1) * LANES]
            ref[index + (q, slice(row, row + value.shape[0]), slice(None))] = part

    def load_rows(ref, index, row, count):
        parts = [ref[index + (q, slice(row, row + count), slice(None))] for q in range(quarter)]
        return jnp.concatenate(parts, axis=1)

    loads = []
    for t in range(share):
        for c in range(3):
            loads.append(
                pltpu.make_async_copy(
                    start_hbm.at[sec * share + t, c],
                    exit_buf.at[0, t, c],
                    load_sem.at[0, t, c],
                )
            )
        loads.append(
            pltpu.make_async_copy(
                start_hbm.at[sec * share + t, pl.ds(3, 3)], vel.at[t], load_sem.at[1, t, 0]
            )
        )
        loads.append(
            pltpu.make_async_copy(cot_hbm.at[sec * share + t], adj.at[t], load_sem.at[1, t, 1])
        )
    for copy in loads:
        copy.start()

    above_out[...] = stiff_ref[1, rows - 1 : rows, :]
    above_in[...] = jnp.zeros_like(above_in)
    upper_in[...] = jnp.zeros_like(upper_in)
    halo_in[...] = jnp.zeros_like(halo_in)
    back_in[...] = jnp.zeros_like(back_in)
    gath[...] = jnp.zeros_like(gath)
    lists_all[sec] = lists_ref[...]
    barrier = pltpu.get_barrier_semaphore()
    for k in range(1, sections):
        pl.semaphore_signal(barrier, inc=1, device_id=(peer(k), spc), device_id_type=MESH)

    @pl.when(has_up)
    def _():
        pl.semaphore_signal(barrier, inc=1, device_id=(sec, spc - 1), device_id_type=MESH)

    @pl.when(has_down)
    def _():
        pl.semaphore_signal(barrier, inc=1, device_id=(sec, spc + 1), device_id_type=MESH)

    for copy in loads:
        copy.wait()
    for t in range(share):
        for c in range(3):
            now = exit_buf[0, t, c]
            store_rows(ext, (0, t, c), 0, now)
            halo_out[0, t, 0, c : c + 1, :] = now[0:1]
            halo_out[0, t, 1, c : c + 1, :] = now[rows - 1 : rows]

    greeted = jnp.where(has_up, 1, 0) + jnp.where(has_down, 1, 0)
    pl.semaphore_wait(barrier, sections - 1 + greeted)

    def to_up(out, into, send, recv, g, t):
        return remote(
            out.at[g, t, 0], into.at[g, t, 1], send.at[g, t, 0], recv.at[g, t, 1], (sec, spc - 1)
        )

    def to_down(out, into, send, recv, g, t):
        return remote(
            out.at[g, t, 1], into.at[g, t, 0], send.at[g, t, 1], recv.at[g, t, 0], (sec, spc + 1)
        )

    halo = (halo_out, halo_in, halo_send, halo_recv)
    back = (back_out, back_in, back_send, back_recv)

    def exchange(kind, g, t):
        @pl.when(has_up)
        def _():
            to_up(*kind, g, t).start()

        @pl.when(has_down)
        def _():
            to_down(*kind, g, t).start()

    def arrive(kind, g, t):
        out, into, send, recv = kind

        @pl.when(has_up)
        def _():
            remote(
                out.at[g, t, 1], into.at[g, t, 0], send.at[g, t, 1], recv.at[g, t, 0], (sec, spc - 1)
            ).wait_recv()

        @pl.when(has_down)
        def _():
            remote(
                out.at[g, t, 0], into.at[g, t, 1], send.at[g, t, 0], recv.at[g, t, 1], (sec, spc + 1)
            ).wait_recv()

    def sent(kind, g, t):
        @pl.when(has_up)
        def _():
            to_up(*kind, g, t).wait_send()

        @pl.when(has_down)
        def _():
            to_down(*kind, g, t).wait_send()

    list_copies = [
        remote(
            lists_ref,
            lists_all.at[sec],
            list_send.at[k - 1],
            list_recv.at[k - 1],
            (peer(k), spc),
        )
        for k in range(1, sections)
    ]
    for copy in list_copies:
        copy.start()
    for t in range(share):
        exchange(halo, 0, t)

    def above_copy():
        return remote(above_out, above_in, above_send, above_recv, (sec, spc + 1))

    @pl.when(has_down)
    def _():
        above_copy().start()

    for copy in list_copies:
        copy.wait()
    to_scalar = pltpu.make_async_copy(lists_all, lists_s, smem_sem)
    to_scalar.start()
    to_scalar.wait()

    @pl.when(has_down)
    def _():
        above_copy().wait_send()

    @pl.when(has_up)
    def _():
        remote(above_out, above_in, above_send, above_recv, (sec, spc - 1)).wait_recv()

    column_mask = (lane_id < width - 1).astype(jnp.float32)
    row_mask = jnp.where(
        jnp.logical_and(last_row, spc * rows + row_id == spaces * rows - 1), 0.0, 1.0
    )

    def right_of(value):
        return pltpu.roll(value, width - 1, 1)

    def left_of(value):
        return pltpu.roll(value, 1, 1)

    def below(value):
        return pltpu.roll(value, rows - 1, 0)

    def above(value):
        return pltpu.roll(value, 1, 0)

    def square(d):
        return d[0] * d[0] + d[1] * d[1] + d[2] * d[2]

    def contact_slot(g, t, p):
        ordinal = g // steps_section
        inner = lax.rem(g, steps_section)
        first = lists_s[ordinal, inner, p]
        second = lists_s[ordinal, inner, pairs + p]
        live = jnp.where(p < lists_s[ordinal, inner, 2 * pairs], 1.0, 0.0)
        return first, second, live

    def tile_rows(ref, index, row, column):
        return [
            ref[index + (c, column, pl.ds(row, 1), slice(None))]
            for c in range(3)
        ]

    def gather_others(g, t):
        for p in range(pairs):
            _, second, _ = contact_slot(g, t, p)
            row = second // quarter
            column = lax.rem(second, quarter)
            place = jnp.where(
                row == 0, rows, jnp.where(row == rows + 1, rows + 1, row - 1)
            )
            found = tile_rows(ext, (g, t), place, column)
            for c in range(3):
                gath[4 * p + c : 4 * p + c + 1, :] = found[c]
        return gath[...].T

    def wide(value):
        return jnp.concatenate([value] * quarter, axis=1)

    coefficient = 2.0 * contact_scale / kernel_spread

    def forward_one(g, t):
        arrive(halo, g, t)
        for side in range(2):
            for c in range(3):
                store_rows(ext, (g, t, c), rows + side, halo_in[g, t, side, c : c + 1, :])
        x = [load_rows(ext, (g, t, c), 0, rows) for c in range(3)]
        up = [load_rows(ext, (g, t, c), rows, 1) for c in range(3)]
        down = [load_rows(ext, (g, t, c), rows + 1, 1) for c in range(3)]
        k_row = stiff_ref[0] * column_mask
        k_column = stiff_ref[1] * row_mask
        d = [right_of(v) - v for v in x]
        pull = k_row * (1.0 - lax.rsqrt(square(d) + tiny_length))
        pulls = [pull * v for v in d]
        force = [v - left_of(v) for v in pulls]
        d = [jnp.where(last_row, down[c], below(x[c])) - x[c] for c in range(3)]
        pull = k_column * (1.0 - lax.rsqrt(square(d) + tiny_length))
        pulls = [pull * v for v in d]
        d = [up[c] - x[c][0:1] for c in range(3)]
        pull = above_in[...] * (1.0 - lax.rsqrt(square(d) + tiny_length))
        force = [
            force[c] + pulls[c] + jnp.where(first_row, pull * d[c], -above(pulls[c]))
            for c in range(3)
        ]
        columns = gather_others(g, t)
        for p in range(pairs):
            first, _, live = contact_slot(g, t, p)
            own = tile_rows(ext, (g, t), first // quarter, lax.rem(first, quarter))
            sums = None
            for j in range(0, LANES, CHUNK):
                s = [own[c] - columns[j : j + CHUNK, 4 * p + c : 4 * p + c + 1] for c in range(3)]
                weight = jnp.exp(square(s) * (-1.0 / kernel_spread))
                terms = [weight * v for v in s]
                sums = terms if sums is None else [a + b for a, b in zip(sums, terms)]
            here = tile_id == first
            for c in range(3):
                repulsion = (coefficient * live) * jnp.sum(sums[c], axis=0, keepdims=True)
                force[c] = force[c] + jnp.where(here, wide(repulsion), 0.0)
        force[2] = force[2] - gravity
        ordinal = g // steps_section
        leaving = lax.rem(g, steps_section) == steps_section - 1
        for c in range(3):
            moved = damping * (vel[t, c] + time_step * force[c])
            point = x[c] + time_step * moved
            vel[t, c] = moved
            store_rows(ext, (g + 1, t, c), 0, point)
            halo_out[g + 1, t, 0, c : c + 1, :] = point[0:1]
            halo_out[g + 1, t, 1, c : c + 1, :] = point[rows - 1 : rows]
            exit_buf[ordinal, t, c] = point
            exit_buf[ordinal, t, 3 + c] = moved

        @pl.when(g < steps - 1)
        def _():
            exchange(halo, g + 1, t)

        @pl.when(leaving)
        def _():
            deliver(exit_buf, exit_hbm, exit_send, exit_recv, 0, ordinal, t, 0, 6)

    def deliver(buf, hbm, send, recv, part, ordinal, t, low, count):
        source = buf.at[ordinal, t, pl.ds(low, count)]
        target = hbm.at[0, sec * share + t, pl.ds(low, count)]

        @pl.when(ordinal == sec)
        def _():
            pltpu.make_async_copy(source, target, send.at[ordinal, t, part]).start()

        @pl.when(ordinal != sec)
        def _():
            remote(
                source, target, send.at[ordinal, t, part], recv.at[sec, t, part], (ordinal, spc)
            ).start()

    def delivered(buf, hbm, send, recv, part, t, low, count):
        for k in range(sections):
            source = buf.at[k, t, pl.ds(low, count)]
            target = hbm.at[0, k * share + t, pl.ds(low, count)]

            @pl.when(sec == k)
            def _():
                pltpu.make_async_copy(source, target, send.at[k, t, part]).wait()

            @pl.when(sec != k)
            def _():
                copy = remote(source, target, send.at[k, t, part], recv.at[k, t, part], (k, spc))
                copy.wait_send()
                copy.wait_recv()

    def forward_step(g, carry):
        for t in range(share):
            forward_one(g, t)
        return carry

    lax.fori_loop(0, steps, forward_step, 0)

    def finish(g, t):
        arrive(back, g, t)
        for c in range(3):
            value = adj[t, c]
            value = value + jnp.where(
                first_row,
                back_in[g, t, 0, c : c + 1, :],
                jnp.where(last_row, back_in[g, t, 1, c : c + 1, :], 0.0),
            )
            adj[t, c] = value
            adj_buf[g // steps_section, t, c] = value

        @pl.when(lax.rem(g, steps_section) == 0)
        def _():
            deliver(adj_buf, adj_hbm, adj_send, adj_recv, 0, g // steps_section, t, 0, 3)

    def back_one(g, t, grads):
        grad_row, grad_column, grad_upper = grads

        @pl.when(g < steps - 1)
        def _():
            finish(g + 1, t)

        point_adj = [adj[t, c] for c in range(3)]
        f = []
        ordinal = g // steps_section
        for c in range(3):
            passed = damping * (adj[t, 3 + c] + time_step * point_adj[c])
            adj[t, 3 + c] = passed
            adj_buf[ordinal, t, 3 + c] = passed
            f.append(time_step * passed)
        for c in range(3):
            store_rows(force_adj, (t, c), 0, f[c])

        @pl.when(lax.rem(g, steps_section) == 0)
        def _():
            deliver(adj_buf, adj_hbm, adj_send, adj_recv, 1, ordinal, t, 3, 3)

        x = [load_rows(ext, (g, t, c), 0, rows) for c in range(3)]
        up = [load_rows(ext, (g, t, c), rows, 1) for c in range(3)]
        down = [load_rows(ext, (g, t, c), rows + 1, 1) for c in range(3)]

        def edge(d, phi, constant):
            inverse = lax.rsqrt(square(d) + tiny_length)
            bend = 1.0 - inverse
            along = d[0] * phi[0] + d[1] * phi[1] + d[2] * phi[2]
            twist = inverse * inverse * inverse * along
            return bend * along, [constant * (bend * phi[c] + twist * d[c]) for c in range(3)]

        d = [right_of(v) - v for v in x]
        part, offset = edge(d, [v - right_of(v) for v in f], stiff_ref[0] * column_mask)
        grad_row = grad_row + part
        out = [point_adj[c] - offset[c] + left_of(offset[c]) for c in range(3)]
        d = [jnp.where(last_row, down[c], below(x[c])) - x[c] for c in range(3)]
        phi = [v - jnp.where(last_row, 0.0, below(v)) for v in f]
        part, offset = edge(d, phi, stiff_ref[1] * row_mask)
        grad_column = grad_column + part
        down_adj = [offset[c][rows - 1 : rows] for c in range(3)]
        d = [up[c] - x[c][0:1] for c in range(3)]
        part, up_adj = edge(d, [v[0:1] for v in f], above_in[...])
        grad_upper = grad_upper + part
        out = [
            out[c] - offset[c] + jnp.where(first_row, -up_adj[c], above(offset[c]))
            for c in range(3)
        ]
        columns = gather_others(g, t)
        ghost = [jnp.zeros((rows, width), jnp.float32) for _ in range(3)]
        for p in range(pairs):
            first, second, live = contact_slot(g, t, p)
            row, column = first // quarter, lax.rem(first, quarter)
            own = tile_rows(ext, (g, t), row, column)
            scale = coefficient * live
            pulled = [scale * v for v in tile_rows(force_adj, (t,), row, column)]
            sums = None
            across = []
            for j in range(0, LANES, CHUNK):
                s = [own[c] - columns[j : j + CHUNK, 4 * p + c : 4 * p + c + 1] for c in range(3)]
                weight = jnp.exp(square(s) * (-1.0 / kernel_spread))
                along = s[0] * pulled[0] + s[1] * pulled[1] + s[2] * pulled[2]
                terms = [weight * (pulled[c] - along * s[c]) for c in range(3)]
                sums = terms if sums is None else [a + b for a, b in zip(sums, terms)]
                across.append([jnp.sum(v, axis=1, keepdims=True) for v in terms])
            here = tile_id == first
            there = tile_id == second - quarter
            outside = halo_tile == second
            for c in range(3):
                gain = wide(jnp.sum(sums[c], axis=0, keepdims=True))
                loss = jnp.concatenate([a[c] for a in across], axis=0)
                loss = wide(jnp.broadcast_to(loss, (LANES, 8)).T[0:1])
                out[c] = out[c] + jnp.where(here, gain, 0.0) - jnp.where(there, loss, 0.0)
                ghost[c] = ghost[c] - jnp.where(outside, loss, 0.0)
        for c in range(3):
            adj[t, c] = out[c]
            back_out[g, t, 0, c : c + 1, :] = up_adj[c] + ghost[c][0:1]
            back_out[g, t, 1, c : c + 1, :] = down_adj[c] + ghost[c][1:2]
        exchange(back, g, t)
        return grad_row, grad_column, grad_upper

    def back_step(i, grads):
        for t in range(share):
            grads = back_one(steps - 1 - i, t, grads)
        return grads

    zero = jnp.zeros((rows, width), jnp.float32)
    grad_row, grad_column, grad_upper = lax.fori_loop(
        0, steps, back_step, (zero, zero, jnp.zeros((1, width), jnp.float32))
    )

    upper_out[...] = grad_upper

    def upper_copy(to):
        return remote(upper_out, upper_in, upper_send, upper_recv, (sec, to))

    @pl.when(has_up)
    def _():
        upper_copy(spc - 1).start()

    @pl.when(has_down)
    def _():
        upper_copy(spc + 1).wait_recv()

    grad_column = grad_column + jnp.where(last_row, upper_in[...], 0.0)
    grad_parts[sec, 0] = grad_row * column_mask
    grad_parts[sec, 1] = grad_column * row_mask
    grad_copies = [
        remote(
            grad_parts.at[sec],
            grad_parts.at[sec],
            grad_send.at[k - 1],
            grad_recv.at[k - 1],
            (peer(k), spc),
        )
        for k in range(1, sections)
    ]
    for copy in grad_copies:
        copy.start()
    for t in range(share):
        finish(0, t)
    for k in range(1, sections):
        other = lax.rem(sec + sections - k, sections)
        remote(
            grad_parts.at[sec],
            grad_parts.at[other],
            grad_send.at[k - 1],
            grad_recv.at[k - 1],
            (peer(k), spc),
        ).wait()
    for c in range(2):
        grad_ref[c] = total([grad_parts[k, c] for k in range(sections)])

    @pl.when(has_up)
    def _():
        upper_copy(spc - 1).wait_send()

    def drain(g, carry):
        for t in range(share):
            sent(halo, g, t)
            sent(back, g, t)
        return carry

    lax.fori_loop(0, steps, drain, 0)
    for t in range(share):
        delivered(exit_buf, exit_hbm, exit_send, exit_recv, 0, t, 0, 6)
        delivered(adj_buf, adj_hbm, adj_send, adj_recv, 1, t, 3, 3)
        delivered(adj_buf, adj_hbm, adj_send, adj_recv, 0, t, 0, 3)


def on_device(start_state, stiffness, contact_a, contact_b, pair_count, cotangent):
    sections, spaces = lax.axis_size("section"), lax.axis_size("space")
    micro, parts, rows, width = start_state.shape
    steps_section, _, pairs = contact_a.shape
    share = micro // sections
    steps = sections * steps_section
    lists = jnp.concatenate([contact_a[:, 0], contact_b[:, 0], pair_count], axis=1)
    lists = jnp.pad(lists, ((0, 8 - steps_section), (0, LANES - lists.shape[1])))
    dims = (sections, spaces, share, steps_section, pairs, rows, width)
    dma = pltpu.SemaphoreType.DMA
    f32 = jnp.float32
    out_state = jax.ShapeDtypeStruct((1, micro, parts, rows, width), f32)
    anywhere = pl.BlockSpec(memory_space=pl.ANY)
    vmem = pl.BlockSpec(memory_space=pltpu.VMEM)
    return pl.pallas_call(
        functools.partial(kernel, dims),
        out_shape=(out_state, out_state, jax.ShapeDtypeStruct((2, rows, width), f32)),
        in_specs=[anywhere, vmem, vmem, anywhere],
        out_specs=(anywhere, anywhere, vmem),
        scratch_shapes=[
            pltpu.VMEM((sections, 8, LANES), jnp.int32),
            pltpu.SMEM((sections, 8, LANES), jnp.int32),
            pltpu.VMEM((steps + 1, share, 3, width // LANES, 2 * rows, LANES), f32),
            pltpu.VMEM((share, 3, rows, width), f32),
            pltpu.VMEM((share, parts, rows, width), f32),
            pltpu.VMEM((sections, share, parts, rows, width), f32),
            pltpu.VMEM((sections, share, parts, rows, width), f32),
            pltpu.VMEM((steps + 1, share, 2, 3, width), f32),
            pltpu.VMEM((steps, share, 2, 3, width), f32),
            pltpu.VMEM((steps, share, 2, 3, width), f32),
            pltpu.VMEM((steps, share, 2, 3, width), f32),
            pltpu.VMEM((1, width), f32),
            pltpu.VMEM((1, width), f32),
            pltpu.VMEM((1, width), f32),
            pltpu.VMEM((1, width), f32),
            pltpu.VMEM((sections, 2, rows, width), f32),
            pltpu.VMEM((LANES, LANES), f32),
            pltpu.VMEM((share, 3, width // LANES, rows, LANES), f32),
            dma((2, share, 3)),
            dma,
            dma((sections - 1,)),
            dma((sections - 1,)),
            dma((steps, share, 2)),
            dma((steps, share, 2)),
            dma((steps, share, 2)),
            dma((steps, share, 2)),
            dma,
            dma,
            dma,
            dma,
            dma((sections, share, 1)),
            dma((sections, share, 1)),
            dma((sections, share, 2)),
            dma((sections, share, 2)),
            dma((sections - 1,)),
            dma((sections - 1,)),
        ],
        compiler_params=pltpu.CompilerParams(collective_id=0, has_side_effects=True),
    )(start_state, stiffness, lists, cotangent)


def solution(mesh):
    in_specs = (
        P(None, None, "space", None),
        P(None, "space", None),
        P("section", "space", None),
        P("section", "space", None),
        P("section", "space"),
        P(None, None, "space", None),
    )
    out_specs = (
        P("section", None, None, "space", None),
        P("section", None, None, "space", None),
        P(None, "space", None),
    )
    return jax.shard_map(
        on_device, mesh=mesh, in_specs=in_specs, out_specs=out_specs, check_vma=False
    )
```

```python
import functools
import math

import jax
import jax.numpy as jnp
from jax import lax
from jax.experimental import pallas as pl
from jax.experimental.pallas import tpu as pltpu
from jax.sharding import PartitionSpec as P

time_step = 0.1
damping = 0.98
contact_scale = 0.3
kernel_spread = 2.0
gravity = 0.5
tiny_length = 1e-06
LANES = 128
DEPTH = 8
MESH = pl.DeviceIdType.MESH


def total(parts):
    result = parts[0]
    for part in parts[1:]:
        result = result + part
    return result


def kernel(
    dims,
    start_hbm,
    stiff_ref,
    lists_ref,
    cot_hbm,
    exit_hbm,
    adj_hbm,
    grad_ref,
    lists_all,
    lists_s,
    ext,
    halo_in,
    vel,
    adj,
    exit_buf,
    adj_buf,
    back_out,
    back_in,
    above_out,
    above_in,
    upper_out,
    upper_in,
    grad_parts,
    force_adj,
    load_sem,
    smem_sem,
    list_send,
    list_recv,
    halo_send,
    halo_recv,
    back_send,
    back_recv,
    above_send,
    above_recv,
    upper_send,
    upper_recv,
    exit_send,
    exit_recv,
    adj_send,
    adj_recv,
    grad_send,
    grad_recv,
):
    sections, spaces, share, steps_section, pairs, rows, width = dims
    steps = sections * steps_section
    quarter = width // LANES
    sec = lax.axis_index("section")
    spc = lax.axis_index("space")
    has_up = spc > 0
    has_down = spc < spaces - 1

    row_id = lax.broadcasted_iota(jnp.int32, (rows, width), 0)
    lane_id = lax.broadcasted_iota(jnp.int32, (rows, width), 1)
    tile_in_row = lax.shift_right_logical(lane_id, LANES.bit_length() - 1)
    tile_id = row_id * quarter + tile_in_row
    first_row = row_id == 0
    last_row = row_id == rows - 1
    halo_tile = jnp.where(
        first_row,
        tile_in_row,
        jnp.where(row_id == 1, tile_in_row + (rows + 1) * quarter, -1),
    )

    def remote(src, dst, send, recv, device):
        return pltpu.make_async_remote_copy(
            src_ref=src,
            dst_ref=dst,
            send_sem=send,
            recv_sem=recv,
            device_id=device,
            device_id_type=MESH,
        )

    def peer(k):
        return lax.rem(sec + k, sections)

    def store_rows(ref, index, lead, part, value):
        for q in range(quarter):
            ref[index + (pl.ds((lead + q) * DEPTH + part, rows, stride=quarter * DEPTH), slice(None))] = (
                value[:, q * LANES : (q + 1) * LANES]
            )

    def load_rows(ref, index, lead, part, count):
        parts = []
        for q in range(quarter):
            at = (lead + q) * DEPTH + part
            where = pl.ds(at, 1) if count == 1 else pl.ds(at, count, stride=quarter * DEPTH)
            parts.append(ref[index + (where, slice(None))])
        return jnp.concatenate(parts, axis=1)

    def store_points(g, t, x):
        for c in range(3):
            store_rows(ext, (g, t), quarter, c, x[c])
        store_rows(ext, (g, t), quarter, 3, square(x))

    def square(d):
        return d[0] * d[0] + d[1] * d[1] + d[2] * d[2]

    loads = []
    for t in range(share):
        for c in range(3):
            loads.append(
                pltpu.make_async_copy(
                    start_hbm.at[sec * share + t, c],
                    exit_buf.at[0, t, c],
                    load_sem.at[0, t, c],
                )
            )
        loads.append(
            pltpu.make_async_copy(
                start_hbm.at[sec * share + t, pl.ds(3, 3)], vel.at[t], load_sem.at[1, t, 0]
            )
        )
        loads.append(
            pltpu.make_async_copy(cot_hbm.at[sec * share + t], adj.at[t], load_sem.at[1, t, 1])
        )
    for copy in loads:
        copy.start()

    above_out[...] = stiff_ref[1, rows - 1 : rows, :]
    above_in[...] = jnp.zeros_like(above_in)
    upper_in[...] = jnp.zeros_like(upper_in)
    band = quarter * DEPTH
    halo_in[...] = jnp.zeros_like(halo_in)
    back_in[...] = jnp.zeros_like(back_in)
    lists_all[sec] = lists_ref[...]
    barrier = pltpu.get_barrier_semaphore()
    for k in range(1, sections):
        pl.semaphore_signal(barrier, inc=1, device_id=(peer(k), spc), device_id_type=MESH)

    @pl.when(has_up)
    def _():
        pl.semaphore_signal(barrier, inc=1, device_id=(sec, spc - 1), device_id_type=MESH)

    @pl.when(has_down)
    def _():
        pl.semaphore_signal(barrier, inc=1, device_id=(sec, spc + 1), device_id_type=MESH)

    for copy in loads:
        copy.wait()
    for t in range(share):
        store_points(0, t, [exit_buf[0, t, c] for c in range(3)])

    greeted = jnp.where(has_up, 1, 0) + jnp.where(has_down, 1, 0)
    pl.semaphore_wait(barrier, sections - 1 + greeted)

    def part_of(ref, g, t, side):
        if ref is not ext:
            return ref.at[g, t, side]
        return ref.at[g, t, pl.ds(band * (1 if side == 0 else rows), band)]

    def to_up(out, into, send, recv, g, t):
        source, target = part_of(out, g, t, 0), part_of(into, g, t, 1)
        return remote(source, target, send.at[g, t, 0], recv.at[g, t, 1], (sec, spc - 1))

    def to_down(out, into, send, recv, g, t):
        source, target = part_of(out, g, t, 1), part_of(into, g, t, 0)
        return remote(source, target, send.at[g, t, 1], recv.at[g, t, 0], (sec, spc + 1))

    halo = (ext, halo_in, halo_send, halo_recv)
    back = (back_out, back_in, back_send, back_recv)

    def exchange(kind, g, t):
        @pl.when(has_up)
        def _():
            to_up(*kind, g, t).start()

        @pl.when(has_down)
        def _():
            to_down(*kind, g, t).start()

    def arrive(kind, g, t):
        out, into, send, recv = kind

        @pl.when(has_up)
        def _():
            source, target = part_of(out, g, t, 1), part_of(into, g, t, 0)
            remote(source, target, send.at[g, t, 1], recv.at[g, t, 0], (sec, spc - 1)).wait_recv()

        @pl.when(has_down)
        def _():
            source, target = part_of(out, g, t, 0), part_of(into, g, t, 1)
            remote(source, target, send.at[g, t, 0], recv.at[g, t, 1], (sec, spc + 1)).wait_recv()

    def sent(kind, g, t):
        @pl.when(has_up)
        def _():
            to_up(*kind, g, t).wait_send()

        @pl.when(has_down)
        def _():
            to_down(*kind, g, t).wait_send()

    list_copies = [
        remote(
            lists_ref,
            lists_all.at[sec],
            list_send.at[k - 1],
            list_recv.at[k - 1],
            (peer(k), spc),
        )
        for k in range(1, sections)
    ]
    for copy in list_copies:
        copy.start()
    for t in range(share):
        exchange(halo, 0, t)

    def above_copy():
        return remote(above_out, above_in, above_send, above_recv, (sec, spc + 1))

    @pl.when(has_down)
    def _():
        above_copy().start()

    for copy in list_copies:
        copy.wait()
    to_scalar = pltpu.make_async_copy(lists_all, lists_s, smem_sem)
    to_scalar.start()
    to_scalar.wait()

    @pl.when(has_down)
    def _():
        above_copy().wait_send()

    @pl.when(has_up)
    def _():
        remote(above_out, above_in, above_send, above_recv, (sec, spc - 1)).wait_recv()

    column_mask = (lane_id < width - 1).astype(jnp.float32)
    row_mask = jnp.where(
        jnp.logical_and(last_row, spc * rows + row_id == spaces * rows - 1), 0.0, 1.0
    )

    def right_of(value):
        return pltpu.roll(value, width - 1, 1)

    def left_of(value):
        return pltpu.roll(value, 1, 1)

    def below(value):
        return pltpu.roll(value, rows - 1, 0)

    def above(value):
        return pltpu.roll(value, 1, 0)

    def contact_slot(g, t, p):
        ordinal = g // steps_section
        inner = lax.rem(g, steps_section)
        first = lists_s[ordinal, inner, p]
        second = lists_s[ordinal, inner, pairs + p]
        live = jnp.where(p < lists_s[ordinal, inner, 2 * pairs], 1.0, 0.0)
        return first, second, live

    part_id = lax.broadcasted_iota(jnp.int32, (DEPTH, LANES), 0)

    def block(ref, index, tile):
        at = tile * DEPTH
        return ref[index + (pl.ds(at, DEPTH), slice(None))]

    def point_block(g, t, tile):
        found = block(ext, (g, t), tile)
        return jnp.where(part_id < 4, found, jnp.where(part_id == 4, 1.0, 0.0))

    def pieces(value):
        one = value.astype(jnp.bfloat16).astype(jnp.float32)
        rest = value - one
        two = rest.astype(jnp.bfloat16).astype(jnp.float32)
        return one, two, rest - two

    def left_stack(u):
        return jnp.concatenate([u[0], u[0], u[1], u[1], u[0], u[2]], axis=0).astype(jnp.bfloat16)

    def right_stack(v):
        return jnp.concatenate([v[0], v[1], v[0], v[1], v[2], v[0]], axis=0).astype(jnp.bfloat16)

    def sum_stack(u):
        whole = jnp.concatenate([u[0], u[1], u[2], jnp.zeros_like(u[0])], axis=0)
        whole = whole.astype(jnp.bfloat16)
        return jnp.concatenate([whole, whole], axis=1)

    def halves(value):
        one = value.astype(jnp.bfloat16)
        return one, (value - one.astype(jnp.float32)).astype(jnp.bfloat16)

    def multiply(left, right, over_left, over_right):
        return lax.dot_general(
            left,
            right,
            (((over_left,), (over_right,)), ((), ())),
            preferred_element_type=jnp.float32,
        )

    def folded(value):
        return value[0:DEPTH] + value[DEPTH : 2 * DEPTH] + value[2 * DEPTH : 3 * DEPTH]

    def over_others(stack, parts):
        return folded(multiply(stack, jnp.concatenate(parts, axis=0), 1, 0))

    def over_own(stack, parts):
        return folded(multiply(stack, jnp.concatenate(parts, axis=1), 1, 1))

    power = -1.0 / (kernel_spread * math.log(2.0))

    def distance_block(own):
        return jnp.where(
            part_id < 3,
            own * (-2.0 * power),
            jnp.where(part_id == 3, power, jnp.where(part_id == 4, own[3:4] * power, 0.0)),
        )

    def wide(value):
        return jnp.concatenate([value] * quarter, axis=1)

    coefficient = 2.0 * contact_scale / kernel_spread

    def forward_one(g, t):
        arrive(halo, g, t)
        ext[g, t, 0:band, :] = halo_in[g, t, 0]
        ext[g, t, (rows + 1) * band : (rows + 2) * band, :] = halo_in[g, t, 1]
        x = [load_rows(ext, (g, t), quarter, c, rows) for c in range(3)]
        up = [load_rows(ext, (g, t), 0, c, 1) for c in range(3)]
        down = [load_rows(ext, (g, t), (rows + 1) * quarter, c, 1) for c in range(3)]
        k_row = stiff_ref[0] * column_mask
        k_column = stiff_ref[1] * row_mask
        d = [right_of(v) - v for v in x]
        pull = k_row * (1.0 - lax.rsqrt(square(d) + tiny_length))
        pulls = [pull * v for v in d]
        force = [v - left_of(v) for v in pulls]
        d = [jnp.where(last_row, down[c], below(x[c])) - x[c] for c in range(3)]
        pull = k_column * (1.0 - lax.rsqrt(square(d) + tiny_length))
        pulls = [pull * v for v in d]
        d = [up[c] - x[c][0:1] for c in range(3)]
        pull = above_in[...] * (1.0 - lax.rsqrt(square(d) + tiny_length))
        force = [
            force[c] + pulls[c] + jnp.where(first_row, pull * d[c], -above(pulls[c]))
            for c in range(3)
        ]
        for p in range(pairs):
            first, second, live = contact_slot(g, t, p)
            own = point_block(g, t, first + quarter)
            other = pieces(point_block(g, t, second))
            weight = jnp.exp2(
                multiply(left_stack(other), right_stack(pieces(distance_block(own))), 0, 0)
            )
            sums = over_others(sum_stack(other), halves(weight))
            repulsion = (coefficient * live) * (own * sums[4:5] - sums)
            here = tile_id == first
            for c in range(3):
                force[c] = force[c] + jnp.where(here, wide(repulsion[c : c + 1]), 0.0)
        force[2] = force[2] - gravity
        ordinal = g // steps_section
        leaving = lax.rem(g, steps_section) == steps_section - 1
        points = []
        for c in range(3):
            moved = damping * (vel[t, c] + time_step * force[c])
            point = x[c] + time_step * moved
            vel[t, c] = moved
            points.append(point)
            exit_buf[ordinal, t, c] = point
            exit_buf[ordinal, t, 3 + c] = moved
        store_points(g + 1, t, points)

        @pl.when(g < steps - 1)
        def _():
            exchange(halo, g + 1, t)

        @pl.when(leaving)
        def _():
            deliver(exit_buf, exit_hbm, exit_send, exit_recv, 0, ordinal, t, 0, 6)

    def deliver(buf, hbm, send, recv, part, ordinal, t, low, count):
        source = buf.at[ordinal, t, pl.ds(low, count)]
        target = hbm.at[0, sec * share + t, pl.ds(low, count)]

        @pl.when(ordinal == sec)
        def _():
            pltpu.make_async_copy(source, target, send.at[ordinal, t, part]).start()

        @pl.when(ordinal != sec)
        def _():
            remote(
                source, target, send.at[ordinal, t, part], recv.at[sec, t, part], (ordinal, spc)
            ).start()

    def delivered(buf, hbm, send, recv, part, t, low, count):
        for k in range(sections):
            source = buf.at[k, t, pl.ds(low, count)]
            target = hbm.at[0, k * share + t, pl.ds(low, count)]

            @pl.when(sec == k)
            def _():
                pltpu.make_async_copy(source, target, send.at[k, t, part]).wait()

            @pl.when(sec != k)
            def _():
                copy = remote(source, target, send.at[k, t, part], recv.at[k, t, part], (k, spc))
                copy.wait_send()
                copy.wait_recv()

    def forward_step(g, carry):
        for t in range(share):
            forward_one(g, t)
        return carry

    lax.fori_loop(0, steps, forward_step, 0)

    def finish(g, t):
        arrive(back, g, t)
        for c in range(3):
            value = adj[t, c]
            value = value + jnp.where(
                first_row,
                back_in[g, t, 0, c : c + 1, :],
                jnp.where(last_row, back_in[g, t, 1, c : c + 1, :], 0.0),
            )
            adj[t, c] = value
            adj_buf[g // steps_section, t, c] = value

        @pl.when(lax.rem(g, steps_section) == 0)
        def _():
            deliver(adj_buf, adj_hbm, adj_send, adj_recv, 0, g // steps_section, t, 0, 3)

    def back_one(g, t, grads):
        grad_row, grad_column, grad_upper = grads

        @pl.when(g < steps - 1)
        def _():
            finish(g + 1, t)

        point_adj = [adj[t, c] for c in range(3)]
        f = []
        ordinal = g // steps_section
        for c in range(3):
            passed = damping * (adj[t, 3 + c] + time_step * point_adj[c])
            adj[t, 3 + c] = passed
            adj_buf[ordinal, t, 3 + c] = passed
            f.append(time_step * passed)
        for c in range(3):
            store_rows(force_adj, (t,), 0, c, f[c])

        @pl.when(lax.rem(g, steps_section) == 0)
        def _():
            deliver(adj_buf, adj_hbm, adj_send, adj_recv, 1, ordinal, t, 3, 3)

        x = [load_rows(ext, (g, t), quarter, c, rows) for c in range(3)]
        up = [load_rows(ext, (g, t), 0, c, 1) for c in range(3)]
        down = [load_rows(ext, (g, t), (rows + 1) * quarter, c, 1) for c in range(3)]

        def edge(d, phi, constant):
            inverse = lax.rsqrt(square(d) + tiny_length)
            bend = 1.0 - inverse
            along = d[0] * phi[0] + d[1] * phi[1] + d[2] * phi[2]
            twist = inverse * inverse * inverse * along
            return bend * along, [constant * (bend * phi[c] + twist * d[c]) for c in range(3)]

        d = [right_of(v) - v for v in x]
        part, offset = edge(d, [v - right_of(v) for v in f], stiff_ref[0] * column_mask)
        grad_row = grad_row + part
        out = [point_adj[c] - offset[c] + left_of(offset[c]) for c in range(3)]
        d = [jnp.where(last_row, down[c], below(x[c])) - x[c] for c in range(3)]
        phi = [v - jnp.where(last_row, 0.0, below(v)) for v in f]
        part, offset = edge(d, phi, stiff_ref[1] * row_mask)
        grad_column = grad_column + part
        down_adj = [offset[c][rows - 1 : rows] for c in range(3)]
        d = [up[c] - x[c][0:1] for c in range(3)]
        part, up_adj = edge(d, [v[0:1] for v in f], above_in[...])
        grad_upper = grad_upper + part
        out = [
            out[c] - offset[c] + jnp.where(first_row, -up_adj[c], above(offset[c]))
            for c in range(3)
        ]
        ghost = [jnp.zeros((rows, width), jnp.float32) for _ in range(3)]
        for p in range(pairs):
            first, second, live = contact_slot(g, t, p)
            own = point_block(g, t, first + quarter)
            other_block = point_block(g, t, second)
            other = pieces(other_block)
            pulled = jnp.where(part_id < 3, (coefficient * live) * block(force_adj, (t,), first), 0.0)
            along = jnp.sum(own * pulled, axis=0, keepdims=True)
            along = jnp.where(part_id == 4, along, -pulled)
            right = jnp.concatenate(
                [right_stack(pieces(distance_block(own))), right_stack(pieces(along))], axis=1
            )
            both = multiply(left_stack(other), right, 0, 0)
            weight = jnp.exp2(both[:, :LANES])
            moment = weight * both[:, LANES:]
            weight_parts, moment_parts = halves(weight), halves(moment)
            stack = sum_stack(other)
            weight_sum = over_others(stack, weight_parts)
            moment_sum = over_others(stack, moment_parts)
            gain = pulled * weight_sum[4:5] - own * moment_sum[4:5] + moment_sum
            weight_sum = over_own(sum_stack(pieces(pulled)), weight_parts)
            moment_sum = over_own(sum_stack(pieces(own)), moment_parts)
            loss = weight_sum - moment_sum + other_block * moment_sum[4:5]
            here = tile_id == first
            there = tile_id == second - quarter
            outside = halo_tile == second
            for c in range(3):
                lost = wide(loss[c : c + 1])
                out[c] = (
                    out[c]
                    + jnp.where(here, wide(gain[c : c + 1]), 0.0)
                    - jnp.where(there, lost, 0.0)
                )
                ghost[c] = ghost[c] - jnp.where(outside, lost, 0.0)
        for c in range(3):
            adj[t, c] = out[c]
            back_out[g, t, 0, c : c + 1, :] = up_adj[c] + ghost[c][0:1]
            back_out[g, t, 1, c : c + 1, :] = down_adj[c] + ghost[c][1:2]
        exchange(back, g, t)
        return grad_row, grad_column, grad_upper

    def back_step(i, grads):
        for t in range(share):
            grads = back_one(steps - 1 - i, t, grads)
        return grads

    zero = jnp.zeros((rows, width), jnp.float32)
    grad_row, grad_column, grad_upper = lax.fori_loop(
        0, steps, back_step, (zero, zero, jnp.zeros((1, width), jnp.float32))
    )

    upper_out[...] = grad_upper

    def upper_copy(to):
        return remote(upper_out, upper_in, upper_send, upper_recv, (sec, to))

    @pl.when(has_up)
    def _():
        upper_copy(spc - 1).start()

    @pl.when(has_down)
    def _():
        upper_copy(spc + 1).wait_recv()

    grad_column = grad_column + jnp.where(last_row, upper_in[...], 0.0)
    grad_parts[sec, 0] = grad_row * column_mask
    grad_parts[sec, 1] = grad_column * row_mask
    grad_copies = [
        remote(
            grad_parts.at[sec],
            grad_parts.at[sec],
            grad_send.at[k - 1],
            grad_recv.at[k - 1],
            (peer(k), spc),
        )
        for k in range(1, sections)
    ]
    for copy in grad_copies:
        copy.start()
    for t in range(share):
        finish(0, t)
    for k in range(1, sections):
        other = lax.rem(sec + sections - k, sections)
        remote(
            grad_parts.at[sec],
            grad_parts.at[other],
            grad_send.at[k - 1],
            grad_recv.at[k - 1],
            (peer(k), spc),
        ).wait()
    for c in range(2):
        grad_ref[c] = total([grad_parts[k, c] for k in range(sections)])

    @pl.when(has_up)
    def _():
        upper_copy(spc - 1).wait_send()

    def drain(g, carry):
        for t in range(share):
            sent(halo, g, t)
            sent(back, g, t)
        return carry

    lax.fori_loop(0, steps, drain, 0)
    for t in range(share):
        delivered(exit_buf, exit_hbm, exit_send, exit_recv, 0, t, 0, 6)
        delivered(adj_buf, adj_hbm, adj_send, adj_recv, 1, t, 3, 3)
        delivered(adj_buf, adj_hbm, adj_send, adj_recv, 0, t, 0, 3)


def on_device(start_state, stiffness, contact_a, contact_b, pair_count, cotangent):
    sections, spaces = lax.axis_size("section"), lax.axis_size("space")
    micro, parts, rows, width = start_state.shape
    steps_section, _, pairs = contact_a.shape
    share = micro // sections
    steps = sections * steps_section
    lists = jnp.concatenate([contact_a[:, 0], contact_b[:, 0], pair_count], axis=1)
    lists = jnp.pad(lists, ((0, 8 - steps_section), (0, LANES - lists.shape[1])))
    dims = (sections, spaces, share, steps_section, pairs, rows, width)
    dma = pltpu.SemaphoreType.DMA
    f32 = jnp.float32
    out_state = jax.ShapeDtypeStruct((1, micro, parts, rows, width), f32)
    anywhere = pl.BlockSpec(memory_space=pl.ANY)
    vmem = pl.BlockSpec(memory_space=pltpu.VMEM)
    return pl.pallas_call(
        functools.partial(kernel, dims),
        out_shape=(out_state, out_state, jax.ShapeDtypeStruct((2, rows, width), f32)),
        in_specs=[anywhere, vmem, vmem, anywhere],
        out_specs=(anywhere, anywhere, vmem),
        scratch_shapes=[
            pltpu.VMEM((sections, 8, LANES), jnp.int32),
            pltpu.SMEM((sections, 8, LANES), jnp.int32),
            pltpu.VMEM((steps + 1, share, (rows + 2) * width // LANES * DEPTH, LANES), f32),
            pltpu.VMEM((steps, share, 2, width // LANES * DEPTH, LANES), f32),
            pltpu.VMEM((share, 3, rows, width), f32),
            pltpu.VMEM((share, parts, rows, width), f32),
            pltpu.VMEM((sections, share, parts, rows, width), f32),
            pltpu.VMEM((sections, share, parts, rows, width), f32),
            pltpu.VMEM((steps, share, 2, 3, width), f32),
            pltpu.VMEM((steps, share, 2, 3, width), f32),
            pltpu.VMEM((1, width), f32),
            pltpu.VMEM((1, width), f32),
            pltpu.VMEM((1, width), f32),
            pltpu.VMEM((1, width), f32),
            pltpu.VMEM((sections, 2, rows, width), f32),
            pltpu.VMEM((share, rows * width // LANES * DEPTH, LANES), f32),
            dma((2, share, 3)),
            dma,
            dma((sections - 1,)),
            dma((sections - 1,)),
            dma((steps, share, 2)),
            dma((steps, share, 2)),
            dma((steps, share, 2)),
            dma((steps, share, 2)),
            dma,
            dma,
            dma,
            dma,
            dma((sections, share, 1)),
            dma((sections, share, 1)),
            dma((sections, share, 2)),
            dma((sections, share, 2)),
            dma((sections - 1,)),
            dma((sections - 1,)),
        ],
        compiler_params=pltpu.CompilerParams(collective_id=0, has_side_effects=True),
    )(start_state, stiffness, lists, cotangent)


def solution(mesh):
    in_specs = (
        P(None, None, "space", None),
        P(None, "space", None),
        P("section", "space", None),
        P("section", "space", None),
        P("section", "space"),
        P(None, None, "space", None),
    )
    out_specs = (
        P("section", None, None, "space", None),
        P("section", None, None, "space", None),
        P(None, "space", None),
    )
    return jax.shard_map(
        on_device, mesh=mesh, in_specs=in_specs, out_specs=out_specs, check_vma=False
    )
```

```python
import functools
import math

import jax
import jax.numpy as jnp
from jax import lax
from jax.experimental import pallas as pl
from jax.experimental.pallas import tpu as pltpu
from jax.sharding import PartitionSpec as P

time_step = 0.1
damping = 0.98
contact_scale = 0.3
kernel_spread = 2.0
gravity = 0.5
tiny_length = 1e-06
LANES = 128
DEPTH = 8
MESH = pl.DeviceIdType.MESH


def total(parts):
    result = parts[0]
    for part in parts[1:]:
        result = result + part
    return result


def kernel(
    dims,
    start_hbm,
    stiff_ref,
    lists_ref,
    cot_hbm,
    exit_hbm,
    adj_hbm,
    grad_ref,
    lists_all,
    lists_s,
    ext,
    halo_in,
    vel,
    adj,
    exit_buf,
    adj_buf,
    back_out,
    back_in,
    above_out,
    above_in,
    upper_out,
    upper_in,
    grad_parts,
    force_adj,
    scat,
    load_sem,
    smem_sem,
    list_send,
    list_recv,
    halo_send,
    halo_recv,
    back_send,
    back_recv,
    above_send,
    above_recv,
    upper_send,
    upper_recv,
    exit_send,
    exit_recv,
    adj_send,
    adj_recv,
    grad_send,
    grad_recv,
):
    sections, spaces, share, steps_section, pairs, rows, width = dims
    steps = sections * steps_section
    quarter = width // LANES
    sec = lax.axis_index("section")
    spc = lax.axis_index("space")
    has_up = spc > 0
    has_down = spc < spaces - 1

    row_id = lax.broadcasted_iota(jnp.int32, (rows, width), 0)
    lane_id = lax.broadcasted_iota(jnp.int32, (rows, width), 1)
    tile_in_row = lax.shift_right_logical(lane_id, LANES.bit_length() - 1)
    tile_id = row_id * quarter + tile_in_row
    first_row = row_id == 0
    last_row = row_id == rows - 1
    def remote(src, dst, send, recv, device):
        return pltpu.make_async_remote_copy(
            src_ref=src,
            dst_ref=dst,
            send_sem=send,
            recv_sem=recv,
            device_id=device,
            device_id_type=MESH,
        )

    def peer(k):
        return lax.rem(sec + k, sections)

    def store_rows(ref, index, lead, part, value):
        for q in range(quarter):
            ref[index + (pl.ds((lead + q) * DEPTH + part, rows, stride=quarter * DEPTH), slice(None))] = (
                value[:, q * LANES : (q + 1) * LANES]
            )

    def load_rows(ref, index, lead, part, count):
        parts = []
        for q in range(quarter):
            at = (lead + q) * DEPTH + part
            where = pl.ds(at, 1) if count == 1 else pl.ds(at, count, stride=quarter * DEPTH)
            parts.append(ref[index + (where, slice(None))])
        return jnp.concatenate(parts, axis=1)

    def store_points(g, t, x):
        for c in range(3):
            store_rows(ext, (g, t), quarter, c, x[c])
        store_rows(ext, (g, t), quarter, 3, square(x))

    def square(d):
        return d[0] * d[0] + d[1] * d[1] + d[2] * d[2]

    loads = []
    for t in range(share):
        for c in range(3):
            loads.append(
                pltpu.make_async_copy(
                    start_hbm.at[sec * share + t, c],
                    exit_buf.at[0, t, c],
                    load_sem.at[0, t, c],
                )
            )
        loads.append(
            pltpu.make_async_copy(
                start_hbm.at[sec * share + t, pl.ds(3, 3)], vel.at[t], load_sem.at[1, t, 0]
            )
        )
        loads.append(
            pltpu.make_async_copy(cot_hbm.at[sec * share + t], adj.at[t], load_sem.at[1, t, 1])
        )
    for copy in loads:
        copy.start()

    above_out[...] = stiff_ref[1, rows - 1 : rows, :]
    above_in[...] = jnp.zeros_like(above_in)
    upper_in[...] = jnp.zeros_like(upper_in)
    band = quarter * DEPTH
    halo_in[...] = jnp.zeros_like(halo_in)
    back_in[...] = jnp.zeros_like(back_in)
    lists_all[sec] = lists_ref[...]
    barrier = pltpu.get_barrier_semaphore()
    for k in range(1, sections):
        pl.semaphore_signal(barrier, inc=1, device_id=(peer(k), spc), device_id_type=MESH)

    @pl.when(has_up)
    def _():
        pl.semaphore_signal(barrier, inc=1, device_id=(sec, spc - 1), device_id_type=MESH)

    @pl.when(has_down)
    def _():
        pl.semaphore_signal(barrier, inc=1, device_id=(sec, spc + 1), device_id_type=MESH)

    for copy in loads:
        copy.wait()
    for t in range(share):
        store_points(0, t, [exit_buf[0, t, c] for c in range(3)])

    greeted = jnp.where(has_up, 1, 0) + jnp.where(has_down, 1, 0)
    pl.semaphore_wait(barrier, sections - 1 + greeted)

    def part_of(ref, g, t, side):
        if ref is not ext:
            return ref.at[g, t, side]
        return ref.at[g, t, pl.ds(band * (1 if side == 0 else rows), band)]

    def to_up(out, into, send, recv, g, t):
        source, target = part_of(out, g, t, 0), part_of(into, g, t, 1)
        return remote(source, target, send.at[g, t, 0], recv.at[g, t, 1], (sec, spc - 1))

    def to_down(out, into, send, recv, g, t):
        source, target = part_of(out, g, t, 1), part_of(into, g, t, 0)
        return remote(source, target, send.at[g, t, 1], recv.at[g, t, 0], (sec, spc + 1))

    halo = (ext, halo_in, halo_send, halo_recv)
    back = (back_out, back_in, back_send, back_recv)

    def exchange(kind, g, t):
        @pl.when(has_up)
        def _():
            to_up(*kind, g, t).start()

        @pl.when(has_down)
        def _():
            to_down(*kind, g, t).start()

    def arrive(kind, g, t):
        out, into, send, recv = kind

        @pl.when(has_up)
        def _():
            source, target = part_of(out, g, t, 1), part_of(into, g, t, 0)
            remote(source, target, send.at[g, t, 1], recv.at[g, t, 0], (sec, spc - 1)).wait_recv()

        @pl.when(has_down)
        def _():
            source, target = part_of(out, g, t, 0), part_of(into, g, t, 1)
            remote(source, target, send.at[g, t, 0], recv.at[g, t, 1], (sec, spc + 1)).wait_recv()

    def sent(kind, g, t):
        @pl.when(has_up)
        def _():
            to_up(*kind, g, t).wait_send()

        @pl.when(has_down)
        def _():
            to_down(*kind, g, t).wait_send()

    list_copies = [
        remote(
            lists_ref,
            lists_all.at[sec],
            list_send.at[k - 1],
            list_recv.at[k - 1],
            (peer(k), spc),
        )
        for k in range(1, sections)
    ]
    for copy in list_copies:
        copy.start()
    for t in range(share):
        exchange(halo, 0, t)

    def above_copy():
        return remote(above_out, above_in, above_send, above_recv, (sec, spc + 1))

    @pl.when(has_down)
    def _():
        above_copy().start()

    for copy in list_copies:
        copy.wait()
    to_scalar = pltpu.make_async_copy(lists_all, lists_s, smem_sem)
    to_scalar.start()
    to_scalar.wait()

    @pl.when(has_down)
    def _():
        above_copy().wait_send()

    @pl.when(has_up)
    def _():
        remote(above_out, above_in, above_send, above_recv, (sec, spc - 1)).wait_recv()

    column_mask = (lane_id < width - 1).astype(jnp.float32)
    row_mask = jnp.where(
        jnp.logical_and(last_row, spc * rows + row_id == spaces * rows - 1), 0.0, 1.0
    )

    def right_of(value):
        return pltpu.roll(value, width - 1, 1)

    def left_of(value):
        return pltpu.roll(value, 1, 1)

    def below(value):
        return pltpu.roll(value, rows - 1, 0)

    def above(value):
        return pltpu.roll(value, 1, 0)

    def contact_slot(g, t, p):
        ordinal = g // steps_section
        inner = lax.rem(g, steps_section)
        first = lists_s[ordinal, inner, p]
        second = lists_s[ordinal, inner, pairs + p]
        live = jnp.where(p < lists_s[ordinal, inner, 2 * pairs], 1.0, 0.0)
        return first, second, live

    part_id = lax.broadcasted_iota(jnp.int32, (DEPTH, LANES), 0)

    def block(ref, index, tile):
        at = tile * DEPTH
        return ref[index + (pl.ds(at, DEPTH), slice(None))]

    def point_block(g, t, tile):
        found = block(ext, (g, t), tile)
        return jnp.where(part_id < 4, found, jnp.where(part_id == 4, 1.0, 0.0))

    def pieces(value):
        one = value.astype(jnp.bfloat16).astype(jnp.float32)
        rest = value - one
        two = rest.astype(jnp.bfloat16).astype(jnp.float32)
        return one, two, rest - two

    def left_stack(u):
        return jnp.concatenate([u[0], u[0], u[1], u[1], u[0], u[2]], axis=0).astype(jnp.bfloat16)

    def right_stack(v):
        return jnp.concatenate([v[0], v[1], v[0], v[1], v[2], v[0]], axis=0).astype(jnp.bfloat16)

    def sum_stack(u):
        whole = jnp.concatenate([u[0], u[1], u[2], jnp.zeros_like(u[0])], axis=0)
        whole = whole.astype(jnp.bfloat16)
        return jnp.concatenate([whole, whole], axis=1)

    def halves(value):
        one = value.astype(jnp.bfloat16)
        return one, (value - one.astype(jnp.float32)).astype(jnp.bfloat16)

    def multiply(left, right, over_left, over_right):
        return lax.dot_general(
            left,
            right,
            (((over_left,), (over_right,)), ((), ())),
            preferred_element_type=jnp.float32,
        )

    def folded(value):
        return value[0:DEPTH] + value[DEPTH : 2 * DEPTH] + value[2 * DEPTH : 3 * DEPTH]

    def over_others(stack, parts):
        return folded(multiply(stack, jnp.concatenate(parts, axis=0), 1, 0))

    def over_own(stack, parts):
        return folded(multiply(stack, jnp.concatenate(parts, axis=1), 1, 1))

    power = -1.0 / (kernel_spread * math.log(2.0))

    def distance_block(own):
        return jnp.where(
            part_id < 3,
            own * (-2.0 * power),
            jnp.where(part_id == 3, power, jnp.where(part_id == 4, own[3:4] * power, 0.0)),
        )

    tiles_all = (rows + 2) * quarter

    def place(blocks, tiles):
        depth = len(blocks) * DEPTH
        lane = lax.broadcasted_iota(jnp.int32, (1, depth), 1)
        slot = lax.shift_right_logical(lane, DEPTH.bit_length() - 1)
        part = jnp.bitwise_and(lane, DEPTH - 1)
        code = jnp.zeros_like(lane)
        for number, tile in enumerate(tiles):
            code = jnp.where(slot == number, tile, code)
        code = jnp.where(part < 3, code + part * tiles_all, -1)
        target = lax.broadcasted_iota(jnp.int32, (3 * tiles_all, depth), 0)
        hits = jnp.where(target == code, 1.0, 0.0)
        hits = jnp.concatenate([hits, hits], axis=1).astype(jnp.bfloat16)
        values = jnp.concatenate(halves(jnp.concatenate(blocks, axis=0)), axis=0)
        scat[...] = multiply(hits, values, 1, 0)

    def placed(c):
        return jnp.concatenate(
            [
                scat[pl.ds(c * tiles_all + quarter + q, rows, stride=quarter), :]
                for q in range(quarter)
            ],
            axis=1,
        )

    def placed_row(c, row):
        at = c * tiles_all + row * quarter
        return jnp.concatenate([scat[at + q : at + q + 1, :] for q in range(quarter)], axis=1)

    coefficient = 2.0 * contact_scale / kernel_spread

    def forward_one(g, t):
        arrive(halo, g, t)
        ext[g, t, 0:band, :] = halo_in[g, t, 0]
        ext[g, t, (rows + 1) * band : (rows + 2) * band, :] = halo_in[g, t, 1]
        given, taken = [], []
        for p in range(pairs):
            first, second, live = contact_slot(g, t, p)
            own = point_block(g, t, first + quarter)
            other = pieces(point_block(g, t, second))
            weight = jnp.exp2(
                multiply(left_stack(other), right_stack(pieces(distance_block(own))), 0, 0)
            )
            sums = over_others(sum_stack(other), halves(weight))
            given.append((coefficient * live) * (own * sums[4:5] - sums))
            taken.append(first + quarter)
        place(given, taken)
        x = [load_rows(ext, (g, t), quarter, c, rows) for c in range(3)]
        up = [load_rows(ext, (g, t), 0, c, 1) for c in range(3)]
        down = [load_rows(ext, (g, t), (rows + 1) * quarter, c, 1) for c in range(3)]
        k_row = stiff_ref[0] * column_mask
        k_column = stiff_ref[1] * row_mask
        d = [right_of(v) - v for v in x]
        pull = k_row * (1.0 - lax.rsqrt(square(d) + tiny_length))
        pulls = [pull * v for v in d]
        force = [v - left_of(v) for v in pulls]
        d = [jnp.where(last_row, down[c], below(x[c])) - x[c] for c in range(3)]
        pull = k_column * (1.0 - lax.rsqrt(square(d) + tiny_length))
        pulls = [pull * v for v in d]
        d = [up[c] - x[c][0:1] for c in range(3)]
        pull = above_in[...] * (1.0 - lax.rsqrt(square(d) + tiny_length))
        force = [
            force[c] + pulls[c] + jnp.where(first_row, pull * d[c], -above(pulls[c])) + placed(c)
            for c in range(3)
        ]
        force[2] = force[2] - gravity
        ordinal = g // steps_section
        leaving = lax.rem(g, steps_section) == steps_section - 1
        points = []
        for c in range(3):
            moved = damping * (vel[t, c] + time_step * force[c])
            point = x[c] + time_step * moved
            vel[t, c] = moved
            points.append(point)
            exit_buf[ordinal, t, c] = point
            exit_buf[ordinal, t, 3 + c] = moved
        store_points(g + 1, t, points)

        @pl.when(g < steps - 1)
        def _():
            exchange(halo, g + 1, t)

        @pl.when(leaving)
        def _():
            deliver(exit_buf, exit_hbm, exit_send, exit_recv, 0, ordinal, t, 0, 6)

    def deliver(buf, hbm, send, recv, part, ordinal, t, low, count):
        source = buf.at[ordinal, t, pl.ds(low, count)]
        target = hbm.at[0, sec * share + t, pl.ds(low, count)]

        @pl.when(ordinal == sec)
        def _():
            pltpu.make_async_copy(source, target, send.at[ordinal, t, part]).start()

        @pl.when(ordinal != sec)
        def _():
            remote(
                source, target, send.at[ordinal, t, part], recv.at[sec, t, part], (ordinal, spc)
            ).start()

    def delivered(buf, hbm, send, recv, part, t, low, count):
        for k in range(sections):
            source = buf.at[k, t, pl.ds(low, count)]
            target = hbm.at[0, k * share + t, pl.ds(low, count)]

            @pl.when(sec == k)
            def _():
                pltpu.make_async_copy(source, target, send.at[k, t, part]).wait()

            @pl.when(sec != k)
            def _():
                copy = remote(source, target, send.at[k, t, part], recv.at[k, t, part], (k, spc))
                copy.wait_send()
                copy.wait_recv()

    def forward_step(g, carry):
        for t in range(share):
            forward_one(g, t)
        return carry

    lax.fori_loop(0, steps, forward_step, 0)

    def finish(g, t):
        arrive(back, g, t)
        for c in range(3):
            value = adj[t, c]
            value = value + jnp.where(
                first_row,
                back_in[g, t, 0, c : c + 1, :],
                jnp.where(last_row, back_in[g, t, 1, c : c + 1, :], 0.0),
            )
            adj[t, c] = value
            adj_buf[g // steps_section, t, c] = value

        @pl.when(lax.rem(g, steps_section) == 0)
        def _():
            deliver(adj_buf, adj_hbm, adj_send, adj_recv, 0, g // steps_section, t, 0, 3)

    def back_one(g, t, grads):
        grad_row, grad_column, grad_upper = grads

        @pl.when(g < steps - 1)
        def _():
            finish(g + 1, t)

        point_adj = [adj[t, c] for c in range(3)]
        f = []
        ordinal = g // steps_section
        for c in range(3):
            passed = damping * (adj[t, 3 + c] + time_step * point_adj[c])
            adj[t, 3 + c] = passed
            adj_buf[ordinal, t, 3 + c] = passed
            f.append(time_step * passed)
        for c in range(3):
            store_rows(force_adj, (t,), 0, c, f[c])

        @pl.when(lax.rem(g, steps_section) == 0)
        def _():
            deliver(adj_buf, adj_hbm, adj_send, adj_recv, 1, ordinal, t, 3, 3)

        gains, losses, receivers, sources = [], [], [], []
        for p in range(pairs):
            first, second, live = contact_slot(g, t, p)
            own = point_block(g, t, first + quarter)
            other_block = point_block(g, t, second)
            other = pieces(other_block)
            pulled = jnp.where(part_id < 3, (coefficient * live) * block(force_adj, (t,), first), 0.0)
            along = jnp.sum(own * pulled, axis=0, keepdims=True)
            along = jnp.where(part_id == 4, along, -pulled)
            right = jnp.concatenate(
                [right_stack(pieces(distance_block(own))), right_stack(pieces(along))], axis=1
            )
            both = multiply(left_stack(other), right, 0, 0)
            weight = jnp.exp2(both[:, :LANES])
            moment = weight * both[:, LANES:]
            weight_parts, moment_parts = halves(weight), halves(moment)
            pair_parts = [
                jnp.concatenate([a, b], axis=1) for a, b in zip(weight_parts, moment_parts)
            ]
            sums = over_others(sum_stack(other), pair_parts)
            weight_sum, moment_sum = sums[:, :LANES], sums[:, LANES:]
            gains.append(pulled * weight_sum[4:5] - own * moment_sum[4:5] + moment_sum)
            stack = jnp.concatenate(
                [sum_stack(pieces(pulled)), sum_stack(pieces(-own))], axis=1
            )
            back_sums = over_own(stack, weight_parts + moment_parts)
            losses.append(other_block * back_sums[4:5] - back_sums)
            receivers.append(first + quarter)
            sources.append(second)
        place(gains + losses, receivers + sources)
        x = [load_rows(ext, (g, t), quarter, c, rows) for c in range(3)]
        up = [load_rows(ext, (g, t), 0, c, 1) for c in range(3)]
        down = [load_rows(ext, (g, t), (rows + 1) * quarter, c, 1) for c in range(3)]

        def edge(d, phi, constant):
            inverse = lax.rsqrt(square(d) + tiny_length)
            bend = 1.0 - inverse
            along = d[0] * phi[0] + d[1] * phi[1] + d[2] * phi[2]
            twist = inverse * inverse * inverse * along
            return bend * along, [constant * (bend * phi[c] + twist * d[c]) for c in range(3)]

        d = [right_of(v) - v for v in x]
        part, offset = edge(d, [v - right_of(v) for v in f], stiff_ref[0] * column_mask)
        grad_row = grad_row + part
        out = [point_adj[c] - offset[c] + left_of(offset[c]) for c in range(3)]
        d = [jnp.where(last_row, down[c], below(x[c])) - x[c] for c in range(3)]
        phi = [v - jnp.where(last_row, 0.0, below(v)) for v in f]
        part, offset = edge(d, phi, stiff_ref[1] * row_mask)
        grad_column = grad_column + part
        down_adj = [offset[c][rows - 1 : rows] for c in range(3)]
        d = [up[c] - x[c][0:1] for c in range(3)]
        part, up_adj = edge(d, [v[0:1] for v in f], above_in[...])
        grad_upper = grad_upper + part
        out = [
            out[c] - offset[c] + jnp.where(first_row, -up_adj[c], above(offset[c])) + placed(c)
            for c in range(3)
        ]
        for c in range(3):
            adj[t, c] = out[c]
            back_out[g, t, 0, c : c + 1, :] = up_adj[c] + placed_row(c, 0)
            back_out[g, t, 1, c : c + 1, :] = down_adj[c] + placed_row(c, rows + 1)
        exchange(back, g, t)
        return grad_row, grad_column, grad_upper

    def back_step(i, grads):
        for t in range(share):
            grads = back_one(steps - 1 - i, t, grads)
        return grads

    zero = jnp.zeros((rows, width), jnp.float32)
    grad_row, grad_column, grad_upper = lax.fori_loop(
        0, steps, back_step, (zero, zero, jnp.zeros((1, width), jnp.float32))
    )

    upper_out[...] = grad_upper

    def upper_copy(to):
        return remote(upper_out, upper_in, upper_send, upper_recv, (sec, to))

    @pl.when(has_up)
    def _():
        upper_copy(spc - 1).start()

    @pl.when(has_down)
    def _():
        upper_copy(spc + 1).wait_recv()

    grad_column = grad_column + jnp.where(last_row, upper_in[...], 0.0)
    grad_parts[sec, 0] = grad_row * column_mask
    grad_parts[sec, 1] = grad_column * row_mask
    grad_copies = [
        remote(
            grad_parts.at[sec],
            grad_parts.at[sec],
            grad_send.at[k - 1],
            grad_recv.at[k - 1],
            (peer(k), spc),
        )
        for k in range(1, sections)
    ]
    for copy in grad_copies:
        copy.start()
    for t in range(share):
        finish(0, t)
    for k in range(1, sections):
        other = lax.rem(sec + sections - k, sections)
        remote(
            grad_parts.at[sec],
            grad_parts.at[other],
            grad_send.at[k - 1],
            grad_recv.at[k - 1],
            (peer(k), spc),
        ).wait()
    for c in range(2):
        grad_ref[c] = total([grad_parts[k, c] for k in range(sections)])

    @pl.when(has_up)
    def _():
        upper_copy(spc - 1).wait_send()

    def drain(g, carry):
        for t in range(share):
            sent(halo, g, t)
            sent(back, g, t)
        return carry

    lax.fori_loop(0, steps, drain, 0)
    for t in range(share):
        delivered(exit_buf, exit_hbm, exit_send, exit_recv, 0, t, 0, 6)
        delivered(adj_buf, adj_hbm, adj_send, adj_recv, 1, t, 3, 3)
        delivered(adj_buf, adj_hbm, adj_send, adj_recv, 0, t, 0, 3)


def on_device(start_state, stiffness, contact_a, contact_b, pair_count, cotangent):
    sections, spaces = lax.axis_size("section"), lax.axis_size("space")
    micro, parts, rows, width = start_state.shape
    steps_section, _, pairs = contact_a.shape
    share = micro // sections
    steps = sections * steps_section
    lists = jnp.concatenate([contact_a[:, 0], contact_b[:, 0], pair_count], axis=1)
    lists = jnp.pad(lists, ((0, 8 - steps_section), (0, LANES - lists.shape[1])))
    dims = (sections, spaces, share, steps_section, pairs, rows, width)
    dma = pltpu.SemaphoreType.DMA
    f32 = jnp.float32
    out_state = jax.ShapeDtypeStruct((1, micro, parts, rows, width), f32)
    anywhere = pl.BlockSpec(memory_space=pl.ANY)
    vmem = pl.BlockSpec(memory_space=pltpu.VMEM)
    return pl.pallas_call(
        functools.partial(kernel, dims),
        out_shape=(out_state, out_state, jax.ShapeDtypeStruct((2, rows, width), f32)),
        in_specs=[anywhere, vmem, vmem, anywhere],
        out_specs=(anywhere, anywhere, vmem),
        scratch_shapes=[
            pltpu.VMEM((sections, 8, LANES), jnp.int32),
            pltpu.SMEM((sections, 8, LANES), jnp.int32),
            pltpu.VMEM((steps + 1, share, (rows + 2) * width // LANES * DEPTH, LANES), f32),
            pltpu.VMEM((steps, share, 2, width // LANES * DEPTH, LANES), f32),
            pltpu.VMEM((share, 3, rows, width), f32),
            pltpu.VMEM((share, parts, rows, width), f32),
            pltpu.VMEM((sections, share, parts, rows, width), f32),
            pltpu.VMEM((sections, share, parts, rows, width), f32),
            pltpu.VMEM((steps, share, 2, 3, width), f32),
            pltpu.VMEM((steps, share, 2, 3, width), f32),
            pltpu.VMEM((1, width), f32),
            pltpu.VMEM((1, width), f32),
            pltpu.VMEM((1, width), f32),
            pltpu.VMEM((1, width), f32),
            pltpu.VMEM((sections, 2, rows, width), f32),
            pltpu.VMEM((share, rows * width // LANES * DEPTH, LANES), f32),
            pltpu.VMEM((3 * (rows + 2) * width // LANES, LANES), f32),
            dma((2, share, 3)),
            dma,
            dma((sections - 1,)),
            dma((sections - 1,)),
            dma((steps, share, 2)),
            dma((steps, share, 2)),
            dma((steps, share, 2)),
            dma((steps, share, 2)),
            dma,
            dma,
            dma,
            dma,
            dma((sections, share, 1)),
            dma((sections, share, 1)),
            dma((sections, share, 2)),
            dma((sections, share, 2)),
            dma((sections - 1,)),
            dma((sections - 1,)),
        ],
        compiler_params=pltpu.CompilerParams(collective_id=0, has_side_effects=True),
    )(start_state, stiffness, lists, cotangent)


def solution(mesh):
    in_specs = (
        P(None, None, "space", None),
        P(None, "space", None),
        P("section", "space", None),
        P("section", "space", None),
        P("section", "space"),
        P(None, None, "space", None),
    )
    out_specs = (
        P("section", None, None, "space", None),
        P("section", None, None, "space", None),
        P(None, "space", None),
    )
    return jax.shard_map(
        on_device, mesh=mesh, in_specs=in_specs, out_specs=out_specs, check_vma=False
    )
```
